512 devices in a mesh: tm: 32 (over z, x_lo), height: 16 (over y, x_hi, core).
Axes of the slice: x: 4 (x_hi: 2, x_lo: 2; x = x_hi * 2 + x_lo), y: 4, z: 16, core: 2. Of those that a mesh axis runs over, the one named last changes fastest.
Arguments:
- frames_in: bfloat16 [512, 128, 1024], P('tm', 'height'), may hold values from -6 to 6
- time_filter: bfloat16 [512, 64], replicated, may hold values from -0.25 to 0.25
- height_filter: bfloat16 [128, 64], replicated, may hold values from -0.5 to 0.5
Outputs:
- layer_out: bfloat16 [512, 128, 1024], P('tm', 'height')
The draws below stay inside these ranges and needn't reach their ends.
All inputs are finite; a program needn't handle non-finite values.
Results may differ from the reference program's by a relative error of at most 0.0051.
Values may be sent and summed in bfloat16 or wider, within the bound.
A program may use at most 64 MiB of HBM per device.

```python
import jax
import jax.numpy as jnp

FRAMES = 512
HEIGHT = 128
CH = 64
LANES = 1024


def block_scale(key, dims, pieces, low, high):
    gain, own = 1.0, jax.random.fold_in(key, 6)
    for axis_at, blocks in pieces:
        steps = jnp.exp(jax.random.uniform(jax.random.fold_in(own, axis_at), (blocks,), jnp.float32, low / len(pieces), high / len(pieces)))
        gain = gain * jnp.repeat(steps, dims[axis_at] // blocks).reshape([-1 if axis == axis_at else 1 for axis in range(len(dims))])
    return gain


def scatter_about(own_key, shape, width, reach, cuts=(), dtype=jnp.bfloat16):
    level = block_scale(own_key, shape, cuts, -0.22, 0.18) if cuts else 1.0
    values = jax.random.normal(own_key, shape, jnp.float32) * width * level
    return jnp.minimum(jnp.maximum(values, -reach), reach).astype(dtype)


def setup_inputs(seed: int = 0) -> dict:
    splits = jax.random.split(jax.random.key(seed), 4)
    frames_in = scatter_about(splits[0], (FRAMES, HEIGHT, LANES), 1.0, 6.0, ((0, 32), (1, 16)))
    time_filter = scatter_about(splits[1], (FRAMES, CH), FRAMES ** -0.5, 0.25)
    height_filter = scatter_about(splits[2], (HEIGHT, CH), HEIGHT ** -0.5, 0.5)
    return dict(frames_in=frames_in, time_filter=time_filter, height_filter=height_filter)


def reference(frames_in, time_filter, height_filter):
    lane_total = frames_in.shape[2]
    across = lane_total // CH
    signal = frames_in.astype(jnp.float32).reshape(FRAMES, HEIGHT, across, CH)
    spectrum = jnp.fft.rfft(signal, axis=0)
    kernel = jnp.fft.rfft(time_filter.astype(jnp.float32), axis=0)[:, None, None, :]
    temporal = jnp.fft.irfft(spectrum * kernel, n=FRAMES, axis=0).astype(jnp.bfloat16)
    row_spectrum = jnp.fft.rfft(temporal.astype(jnp.float32), axis=1)
    row_kernel = jnp.fft.rfft(height_filter.astype(jnp.float32), axis=0)[None, :, None, :]
    spatial = jnp.fft.irfft(row_spectrum * row_kernel, n=HEIGHT, axis=1).astype(jnp.bfloat16)
    spatial = spatial.reshape(FRAMES, HEIGHT, lane_total)
    return (frames_in.astype(jnp.float32) + spatial.astype(jnp.float32)).astype(jnp.bfloat16)
```

```python
import functools

import jax
import jax.numpy as jnp
import numpy as np
from jax import lax
from jax.experimental import pallas as pl
from jax.experimental.pallas import tpu as pltpu
from jax.sharding import PartitionSpec as P

MESH = pl.DeviceIdType.MESH
F32, BF16 = jnp.float32, jnp.bfloat16
LANE = 128
CHUNKS = 2


def dft_tables(size):
    half = size // 2
    angle = 2.0 * np.pi * ((np.arange(half)[:, None] * np.arange(size)[None, :]) % size) / size
    sines = np.sin(angle)
    sines[0] = np.cos(np.pi * np.arange(size))
    table = np.concatenate([np.cos(angle), sines], axis=0)
    high = table.astype(np.float32).astype(jnp.bfloat16)
    low = (table - high.astype(np.float64)).astype(np.float32).astype(jnp.bfloat16)
    forward = np.concatenate([high, low], axis=0)
    inverse = np.stack([high.T, low.T])
    return forward, inverse


def dot(a, b):
    return jnp.dot(a, b, preferred_element_type=F32)


def one_hot(shape, hit):
    rows = lax.broadcasted_iota(jnp.int32, shape, 0)
    cols = lax.broadcasted_iota(jnp.int32, shape, 1)
    return jnp.where(hit(rows, cols), 1.0, 0.0).astype(BF16)


def forward_dft(forward, values):
    size = values.shape[0]
    both = dot(forward[...], values)
    return both[:size] + both[size:]


def inverse_dft(inverse, spectrum):
    lanes = spectrum.shape[1]
    high = spectrum.astype(BF16)
    low = (spectrum - high.astype(F32)).astype(BF16)
    main = dot(inverse[0], jnp.concatenate([high, low], axis=1))
    return main[:, :lanes] + main[:, lanes:] + dot(inverse[1], high)


def store_response(forward, taps, response):
    size, channels = taps.shape
    half = size // 2
    spread = one_hot((channels, LANE), lambda r, c: r == c % channels)
    spectrum = forward_dft(forward, dot(taps[...], spread).astype(BF16))
    first = lax.broadcasted_iota(jnp.int32, (half, LANE), 0) == 0
    scale = jnp.where(first, 1.0 / size, 2.0 / size)
    cosine, sine = spectrum[:half] * scale, spectrum[half:] * scale
    response[0] = cosine
    response[1] = jnp.where(first, 0.0, sine)
    response[2] = jnp.where(first, sine, cosine)


def filtered(forward, inverse, response, values):
    size, lanes = values.shape
    half = size // 2
    spectrum = forward_dft(forward, values)
    cosine, sine = spectrum[:half], spectrum[half:]
    wide = lambda which: jnp.concatenate([response[which]] * (lanes // LANE), axis=1)
    p, q, nyquist_p = wide(0), wide(1), wide(2)
    product = jnp.concatenate([cosine * p - sine * q, cosine * q + sine * nyquist_p], axis=0)
    return inverse_dft(inverse, product)


def kernel(
    tm_count, height_count,
    frames_hbm, time_taps, height_taps, tf_hbm, ti_hbm, hf_hbm, hi_hbm,
    out,
    frames, tf, ti, hf, hi, t_response, h_response,
    t_send, t_have, t_done, t_back, h_send, h_have, h_done, h_back,
    load_sems, own_sems, send_sems, recv_sems,
):
    frames_dev, rows_dev, lane_total = frames.shape
    width = lane_total // CHUNKS
    groups = width // LANE
    block = frames_dev * rows_dev
    tm = lax.axis_index("tm")
    height = lax.axis_index("height")
    z, x_lo = tm // 2, tm % 2
    z_count = tm_count // 2

    loads = [
        pltpu.make_async_copy(src, dst, load_sems.at[i])
        for i, (src, dst) in enumerate(
            [(frames_hbm, frames), (tf_hbm, tf), (ti_hbm, ti), (hf_hbm, hf), (hi_hbm, hi)]
        )
    ]
    for load in loads:
        load.start()

    barrier = pltpu.get_barrier_semaphore()

    def greet_tm(d, carry):
        peer = (tm + d) % tm_count
        pl.semaphore_signal(barrier, inc=1, device_id=(peer, height), device_id_type=MESH)
        return carry

    def greet_height(d, carry):
        peer = (height + d) % height_count
        pl.semaphore_signal(barrier, inc=1, device_id=(tm, peer), device_id_type=MESH)
        return carry

    lax.fori_loop(1, tm_count, greet_tm, 0)
    lax.fori_loop(1, height_count, greet_height, 0)

    loads[0].wait()
    swap_in = one_hot((block, block), lambda r, c: c == (r % frames_dev) * rows_dev + r // frames_dev)
    rows = frames[...].astype(F32).reshape(block, lane_total).astype(BF16)
    turned = dot(swap_in, rows).astype(BF16)
    for c in range(CHUNKS):
        for g in range(groups):
            lo = c * width + g * LANE
            t_send[c, g * rows_dev:(g + 1) * rows_dev] = turned[:, lo:lo + LANE].reshape(
                rows_dev, frames_dev, LANE
            )

    pl.semaphore_wait(barrier, tm_count + height_count - 2)

    def tm_peer(i):
        k = i // 2
        away = z_count // 2 + ((k + 1) // 2) * (1 - 2 * (k % 2))
        return ((z + away) % z_count) * 2 + (x_lo + 1 - i % 2) % 2

    def exchange_tm(phase, c, src, dst):
        pltpu.make_async_copy(src.at[c, tm], dst.at[c, tm], recv_sems.at[phase, c]).start()

        def send(i, carry):
            peer = tm_peer(i)
            pltpu.make_async_remote_copy(
                src_ref=src.at[c, peer], dst_ref=dst.at[c, tm],
                send_sem=send_sems.at[phase, c], recv_sem=recv_sems.at[phase, c],
                device_id=(peer, height), device_id_type=MESH,
            ).start()
            return carry

        lax.fori_loop(0, tm_count - 1, send, 0)

    def exchange_height(phase, c, src, dst):
        pltpu.make_async_copy(src.at[c, height], dst.at[c, height], recv_sems.at[phase, c]).start()

        def send(d, carry):
            peer = (height + d) % height_count
            pltpu.make_async_remote_copy(
                src_ref=src.at[c, peer], dst_ref=dst.at[c, height],
                send_sem=send_sems.at[phase, c], recv_sem=recv_sems.at[phase, c],
                device_id=(tm, peer), device_id_type=MESH,
            ).start()
            return carry

        lax.fori_loop(1, height_count, send, 0)

    def arrived(phase, c, dst):
        pltpu.make_async_copy(dst.at[c], dst.at[c], recv_sems.at[phase, c]).wait()

    def departed(phase, c, src, peers):
        sent = src.at[c, pl.ds(0, peers - 1)]
        pltpu.make_async_copy(sent, sent, send_sems.at[phase, c]).wait()

    for c in range(CHUNKS):
        exchange_tm(0, c, t_send, t_have)

    for load in loads[1:]:
        load.wait()
    store_response(tf, time_taps, t_response)
    store_response(hf, height_taps, h_response)

    def time_stage(c, carry):
        arrived(0, c, t_have)
        values = t_have[c].reshape(tm_count * frames_dev, LANE)
        result = filtered(tf, ti, t_response, values).astype(BF16)
        t_done[c] = result.reshape(tm_count, frames_dev, LANE)
        exchange_tm(1, c, t_done, t_back)
        return carry

    lax.fori_loop(0, CHUNKS, time_stage, 0)

    swap_back = one_hot((block, block), lambda r, c: c == (r % rows_dev) * frames_dev + r // rows_dev)

    def height_stage(c, carry):
        arrived(1, c, t_back)
        for g in range(groups):
            tile = t_back[c, g * rows_dev:(g + 1) * rows_dev].reshape(block, LANE)
            turned = dot(swap_back, tile).reshape(frames_dev, rows_dev, LANE)
            h_send[c, :, :, g * LANE:(g + 1) * LANE] = turned.astype(BF16)
        exchange_height(2, c, h_send, h_have)
        arrived(2, c, h_have)
        values = h_have[c].astype(F32).reshape(height_count * rows_dev, width).astype(BF16)
        result = filtered(hf, hi, h_response, values)
        h_done[c] = result.reshape(height_count, rows_dev, width).astype(BF16)
        exchange_height(3, c, h_done, h_back)
        return carry

    lax.fori_loop(0, CHUNKS, height_stage, 0)

    for c in range(CHUNKS):
        arrived(3, c, h_back)
        lanes = slice(c * width, (c + 1) * width)
        total = frames[:, :, lanes].astype(F32) + h_back[c].astype(F32)
        out[:, :, lanes] = total.astype(BF16)

    for c in range(CHUNKS):
        departed(0, c, t_send, tm_count)
        departed(1, c, t_done, tm_count)
        departed(2, c, h_send, height_count)
        departed(3, c, h_done, height_count)


def shards(frames_in, time_filter, height_filter):
    frames_dev, rows_dev, lane_total = frames_in.shape
    tm_count = lax.axis_size("tm")
    height_count = lax.axis_size("height")
    width = lane_total // CHUNKS
    tf, ti = dft_tables(time_filter.shape[0])
    hf, hi = dft_tables(height_filter.shape[0])
    t_buf = pltpu.VMEM((CHUNKS, tm_count, frames_dev, LANE), BF16)
    h_buf = pltpu.VMEM((CHUNKS, height_count, rows_dev, width), BF16)
    like = lambda a: pltpu.VMEM(a.shape, BF16)
    hbm = pl.BlockSpec(memory_space=pl.ANY)
    vmem = pl.BlockSpec(memory_space=pltpu.VMEM)
    return pl.pallas_call(
        functools.partial(kernel, tm_count, height_count),
        out_shape=jax.ShapeDtypeStruct(frames_in.shape, BF16),
        in_specs=[hbm, vmem, vmem, hbm, hbm, hbm, hbm],
        out_specs=vmem,
        scratch_shapes=[
            pltpu.VMEM(frames_in.shape, BF16),
            like(tf), like(ti), like(hf), like(hi),
            pltpu.VMEM((3, time_filter.shape[0] // 2, LANE), F32),
            pltpu.VMEM((3, height_filter.shape[0] // 2, LANE), F32),
            t_buf, t_buf, t_buf, t_buf, h_buf, h_buf, h_buf, h_buf,
            pltpu.SemaphoreType.DMA((5,)),
            pltpu.SemaphoreType.DMA((1,)),
            pltpu.SemaphoreType.DMA((4, CHUNKS)),
            pltpu.SemaphoreType.DMA((4, CHUNKS)),
        ],
        compiler_params=pltpu.CompilerParams(collective_id=0, has_side_effects=True),
    )(frames_in, time_filter, height_filter, jnp.asarray(tf), jnp.asarray(ti), jnp.asarray(hf), jnp.asarray(hi))


def solution(mesh):
    return jax.shard_map(
        shards,
        mesh=mesh,
        in_specs=(P("tm", "height", None), P(), P()),
        out_specs=P("tm", "height", None),
        check_vma=False,
    )
```

```python
import functools

import jax
import jax.numpy as jnp
import numpy as np
from jax import lax
from jax.experimental import pallas as pl
from jax.experimental.pallas import tpu as pltpu
from jax.sharding import PartitionSpec as P

MESH = pl.DeviceIdType.MESH
F32, BF16 = jnp.float32, jnp.bfloat16
LANE = 128
CHUNKS = 2


def dft_tables(size):
    half = size // 2
    angle = 2.0 * np.pi * ((np.arange(half)[:, None] * np.arange(size)[None, :]) % size) / size
    sines = np.sin(angle)
    sines[0] = np.cos(np.pi * np.arange(size))
    table = np.concatenate([np.cos(angle), sines], axis=0)
    high = table.astype(np.float32).astype(jnp.bfloat16)
    low = (table - high.astype(np.float64)).astype(np.float32).astype(jnp.bfloat16)
    forward = np.concatenate([high, low], axis=0)
    inverse = np.stack([high.T, low.T])
    return forward, inverse


def dot(a, b):
    return jnp.dot(a, b, preferred_element_type=F32)


def one_hot(shape, hit):
    rows = lax.broadcasted_iota(jnp.int32, shape, 0)
    cols = lax.broadcasted_iota(jnp.int32, shape, 1)
    return jnp.where(hit(rows, cols), 1.0, 0.0).astype(BF16)


def forward_dft(forward, values):
    size = values.shape[0]
    both = dot(forward[...], values)
    return both[:size] + both[size:]


def inverse_dft(inverse, spectrum):
    lanes = spectrum.shape[1]
    high = spectrum.astype(BF16)
    low = (spectrum - high.astype(F32)).astype(BF16)
    main = dot(inverse[0], jnp.concatenate([high, low], axis=1))
    return main[:, :lanes] + main[:, lanes:] + dot(inverse[1], high)


def store_response(forward, taps, response):
    channels, size = taps.shape
    half = size // 2
    spread = one_hot((LANE, channels), lambda r, c: c == r % channels)
    wide = dot(spread, taps[...]).astype(BF16)
    both = lax.dot_general(forward[...], wide, (((1,), (1,)), ((), ())), preferred_element_type=F32)
    spectrum = both[:size] + both[size:]
    first = lax.broadcasted_iota(jnp.int32, (half, LANE), 0) == 0
    scale = jnp.where(first, 1.0 / size, 2.0 / size)
    cosine, sine = spectrum[:half] * scale, spectrum[half:] * scale
    response[0] = cosine
    response[1] = jnp.where(first, 0.0, sine)
    response[2] = jnp.where(first, sine, cosine)


def filtered(forward, inverse, response, values):
    size, lanes = values.shape
    half = size // 2
    spectrum = forward_dft(forward, values)
    cosine, sine = spectrum[:half], spectrum[half:]
    wide = lambda which: jnp.concatenate([response[which]] * (lanes // LANE), axis=1)
    p, q, nyquist_p = wide(0), wide(1), wide(2)
    product = jnp.concatenate([cosine * p - sine * q, cosine * q + sine * nyquist_p], axis=0)
    return inverse_dft(inverse, product)


def kernel(
    tm_count, height_count,
    frames_hbm, time_taps, height_taps, tf_hbm, ti_hbm, hf_hbm, hi_hbm,
    out,
    frames, tf, ti, hf, hi, t_response, h_response,
    t_send, t_have, t_done, t_back, h_send, h_have, h_done, h_back,
    load_sems, send_sems, recv_sems,
):
    frames_dev, rows_dev, lane_total = frames.shape
    width = lane_total // CHUNKS
    groups = width // LANE
    block = frames_dev * rows_dev
    tm = lax.axis_index("tm")
    height = lax.axis_index("height")
    z, x_lo = tm // 2, tm % 2
    z_count = tm_count // 2

    loads = [
        pltpu.make_async_copy(src, dst, load_sems.at[i])
        for i, (src, dst) in enumerate(
            [
                (frames_hbm, frames), (tf_hbm, tf), (ti_hbm, ti), (hf_hbm, hf), (hi_hbm, hi),
                (frames_hbm.at[:, :, pl.ds(width, width)], h_send.at[1]),
            ]
        )
    ]
    for load in loads:
        load.start()

    barrier = pltpu.get_barrier_semaphore()

    def greet_tm(d, carry):
        peer = (tm + d) % tm_count
        pl.semaphore_signal(barrier, inc=1, device_id=(peer, height), device_id_type=MESH)
        return carry

    def greet_height(d, carry):
        peer = (height + d) % height_count
        pl.semaphore_signal(barrier, inc=1, device_id=(tm, peer), device_id_type=MESH)
        return carry

    lax.fori_loop(1, tm_count, greet_tm, 0)
    lax.fori_loop(1, height_count, greet_height, 0)

    loads[0].wait()
    swap_in = one_hot((block, block), lambda r, c: c == (r % frames_dev) * rows_dev + r // frames_dev)
    swap_back = one_hot((block, block), lambda r, c: c == (r % rows_dev) * frames_dev + r // rows_dev)

    def rows_first(values, c):
        flat = values.astype(F32).reshape(block, width).astype(BF16)
        turned = dot(swap_in, flat).astype(BF16)
        for g in range(groups):
            t_send[c, g * rows_dev:(g + 1) * rows_dev] = turned[:, g * LANE:(g + 1) * LANE].reshape(
                rows_dev, frames_dev, LANE
            )

    def frames_first(c, g):
        tile = t_back[c, g * rows_dev:(g + 1) * rows_dev].reshape(block, LANE)
        return dot(swap_back, tile).reshape(frames_dev, rows_dev, LANE)

    rows_first(frames[:, :, :width], 0)

    pl.semaphore_wait(barrier, tm_count + height_count - 2)

    def tm_peer(i):
        k = i // 2
        away = z_count // 2 + ((k + 1) // 2) * (1 - 2 * (k % 2))
        return ((z + away) % z_count) * 2 + (x_lo + 1 - i % 2) % 2

    def exchange_tm(phase, c, src, dst):
        pltpu.make_async_copy(src.at[c, tm], dst.at[c, tm], recv_sems.at[phase, c]).start()

        def send(i, carry):
            peer = tm_peer(i)
            pltpu.make_async_remote_copy(
                src_ref=src.at[c, peer], dst_ref=dst.at[c, tm],
                send_sem=send_sems.at[phase, c], recv_sem=recv_sems.at[phase, c],
                device_id=(peer, height), device_id_type=MESH,
            ).start()
            return carry

        lax.fori_loop(0, tm_count - 1, send, 0)

    def exchange_height(phase, c, src, dst):
        pltpu.make_async_copy(src.at[c, height], dst.at[c, height], recv_sems.at[phase, c]).start()

        def send(d, carry):
            peer = (height + d) % height_count
            pltpu.make_async_remote_copy(
                src_ref=src.at[c, peer], dst_ref=dst.at[c, height],
                send_sem=send_sems.at[phase, c], recv_sem=recv_sems.at[phase, c],
                device_id=(tm, peer), device_id_type=MESH,
            ).start()
            return carry

        lax.fori_loop(1, height_count, send, 0)

    def arrived(phase, c, dst):
        pltpu.make_async_copy(dst.at[c], dst.at[c], recv_sems.at[phase, c]).wait()

    def departed(phase, c, src, peers):
        sent = src.at[c, pl.ds(0, peers - 1)]
        pltpu.make_async_copy(sent, sent, send_sems.at[phase, c]).wait()

    def time_stage(c):
        arrived(0, c, t_have)
        values = t_have[c].reshape(tm_count * frames_dev, LANE)
        result = filtered(tf, ti, t_response, values).astype(BF16)
        t_done[c] = result.reshape(tm_count, frames_dev, LANE)
        exchange_tm(1, c, t_done, t_back)

    def height_stage(c):
        arrived(2, c, h_have)
        values = h_have[c].astype(F32).reshape(height_count * rows_dev, width).astype(BF16)
        result = filtered(hf, hi, h_response, values)
        h_done[c] = result.reshape(height_count, rows_dev, width).astype(BF16)
        exchange_height(3, c, h_done, h_back)

    exchange_tm(0, 0, t_send, t_have)
    loads[5].wait()
    exchange_height(2, 1, h_send, h_have)
    for load in loads[1:5]:
        load.wait()
    store_response(hf, height_taps, h_response)
    store_response(tf, time_taps, t_response)

    height_stage(1)
    time_stage(0)

    arrived(3, 1, h_back)
    rows_first(h_back[1], 1)
    exchange_tm(0, 1, t_send, t_have)

    arrived(1, 0, t_back)
    for g in range(groups):
        h_send[0, :, :, g * LANE:(g + 1) * LANE] = frames_first(0, g).astype(BF16)
    exchange_height(2, 0, h_send, h_have)

    time_stage(1)
    height_stage(0)

    arrived(3, 0, h_back)
    out[:, :, :width] = (frames[:, :, :width].astype(F32) + h_back[0].astype(F32)).astype(BF16)

    arrived(1, 1, t_back)
    for g in range(groups):
        lanes = slice(width + g * LANE, width + (g + 1) * LANE)
        out[:, :, lanes] = (frames[:, :, lanes].astype(F32) + frames_first(1, g)).astype(BF16)

    for c in range(CHUNKS):
        departed(0, c, t_send, tm_count)
        departed(1, c, t_done, tm_count)
        departed(2, c, h_send, height_count)
        departed(3, c, h_done, height_count)


def shards(frames_in, time_filter, height_filter):
    frames_dev, rows_dev, lane_total = frames_in.shape
    tm_count = lax.axis_size("tm")
    height_count = lax.axis_size("height")
    width = lane_total // CHUNKS
    tf, ti = dft_tables(time_filter.shape[0])
    hf, hi = dft_tables(height_filter.shape[0])
    t_buf = pltpu.VMEM((CHUNKS, tm_count, frames_dev, LANE), BF16)
    h_buf = pltpu.VMEM((CHUNKS, height_count, rows_dev, width), BF16)
    like = lambda a: pltpu.VMEM(a.shape, BF16)
    hbm = pl.BlockSpec(memory_space=pl.ANY)
    vmem = pl.BlockSpec(memory_space=pltpu.VMEM)
    return pl.pallas_call(
        functools.partial(kernel, tm_count, height_count),
        out_shape=jax.ShapeDtypeStruct(frames_in.shape, BF16),
        in_specs=[hbm, vmem, vmem, hbm, hbm, hbm, hbm],
        out_specs=vmem,
        scratch_shapes=[
            pltpu.VMEM(frames_in.shape, BF16),
            like(tf), like(ti), like(hf), like(hi),
            pltpu.VMEM((3, time_filter.shape[0] // 2, LANE), F32),
            pltpu.VMEM((3, height_filter.shape[0] // 2, LANE), F32),
            t_buf, t_buf, t_buf, t_buf, h_buf, h_buf, h_buf, h_buf,
            pltpu.SemaphoreType.DMA((6,)),
            pltpu.SemaphoreType.DMA((4, CHUNKS)),
            pltpu.SemaphoreType.DMA((4, CHUNKS)),
        ],
        compiler_params=pltpu.CompilerParams(collective_id=0, has_side_effects=True),
    )(frames_in, time_filter.T, height_filter.T, jnp.asarray(tf), jnp.asarray(ti), jnp.asarray(hf), jnp.asarray(hi))


def solution(mesh):
    return jax.shard_map(
        shards,
        mesh=mesh,
        in_specs=(P("tm", "height", None), P(), P()),
        out_specs=P("tm", "height", None),
        check_vma=False,
    )
```

```python
import functools

import jax
import jax.numpy as jnp
import numpy as np
from jax import lax
from jax.experimental import pallas as pl
from jax.experimental.pallas import tpu as pltpu
from jax.sharding import PartitionSpec as P

MESH = pl.DeviceIdType.MESH
F32, BF16 = jnp.float32, jnp.bfloat16
LANE = 128
CHUNKS = 2


def split(table):
    high = table.astype(np.float32).astype(jnp.bfloat16)
    low = (table - high.astype(np.float64)).astype(np.float32).astype(jnp.bfloat16)
    return high, low


def dft_rows(size):
    half = size // 2
    order = np.concatenate([np.arange(0, half, 2), np.arange(1, half, 2)])
    angle = 2.0 * np.pi * ((order[:, None] * np.arange(size)[None, :]) % size) / size
    sines = np.sin(angle)
    sines[0] = np.cos(np.pi * np.arange(size))
    return np.cos(angle), sines


def time_tables(size):
    half, quarter = size // 2, size // 4
    cosines, sines = dft_rows(size)
    parts = [
        np.concatenate([cosines[rows, :half], sines[rows, :half]], axis=0)
        for rows in (slice(0, quarter), slice(quarter, half))
    ]
    forward = np.concatenate(split(np.concatenate(parts, axis=0)), axis=0)
    inverse = np.stack([piece for part in parts for piece in split(part.T)])
    return forward, inverse


def height_tables(size):
    high, low = split(np.concatenate(dft_rows(size), axis=0))
    return np.concatenate([high, low], axis=1), np.concatenate([high.T, low.T], axis=1)


def dot(a, b):
    return jnp.dot(a, b, preferred_element_type=F32)


def halves(values):
    high = values.astype(BF16)
    return high, (values - high.astype(F32)).astype(BF16)


def one_hot(shape, hit):
    rows = lax.broadcasted_iota(jnp.int32, shape, 0)
    cols = lax.broadcasted_iota(jnp.int32, shape, 1)
    return jnp.where(hit(rows, cols), 1.0, 0.0).astype(BF16)


def time_forward(table, values):
    half, quarter = values.shape[0] // 2, values.shape[0] // 4
    both = dot(table[...], jnp.concatenate([values[:half], values[half:]], axis=1))
    both = both[:2 * half] + both[2 * half:]
    even = both[:half, :LANE] + both[:half, LANE:]
    odd = both[half:, :LANE] - both[half:, LANE:]
    cosine = jnp.concatenate([even[:quarter], odd[:quarter]], axis=0)
    sine = jnp.concatenate([even[quarter:], odd[quarter:]], axis=0)
    return cosine, sine


def time_inverse(table, cosine, sine):
    quarter = cosine.shape[0] // 2
    sums = []
    for p in range(2):
        rows = slice(p * quarter, (p + 1) * quarter)
        high, low = halves(jnp.concatenate([cosine[rows], sine[rows]], axis=0))
        main = dot(table[2 * p], jnp.concatenate([high, low], axis=1))
        sums.append(main[:, :LANE] + main[:, LANE:] + dot(table[2 * p + 1], high))
    return jnp.concatenate([sums[0] + sums[1], sums[0] - sums[1]], axis=0)


def height_forward(table, values):
    half = values.shape[0] // 2
    both = dot(table[...], jnp.concatenate([values, values], axis=0))
    return both[:half], both[half:]


def height_inverse(table, cosine, sine):
    high, low = halves(jnp.concatenate([cosine, sine], axis=0))
    return dot(table[...], jnp.concatenate([high, high], axis=0)) + dot(table[:, :high.shape[0]], low)


def store_response(forward, table, taps, response):
    channels, size = taps.shape
    spread = one_hot((LANE, channels), lambda r, c: c == r % channels)
    wide = jnp.transpose(dot(spread, taps[...])).astype(BF16)
    cosine, sine = forward(table, wide)
    first = lax.broadcasted_iota(jnp.int32, cosine.shape, 0) == 0
    scale = jnp.where(first, 1.0 / size, 2.0 / size)
    cosine, sine = cosine * scale, sine * scale
    response[0] = cosine
    response[1] = jnp.where(first, 0.0, sine)
    response[2] = jnp.where(first, sine, cosine)


def product(response, cosine, sine):
    wide = lambda which: jnp.concatenate([response[which]] * (cosine.shape[1] // LANE), axis=1)
    p, q, nyquist_p = wide(0), wide(1), wide(2)
    return cosine * p - sine * q, cosine * q + sine * nyquist_p


def kernel(
    tm_count, height_count,
    frames_hbm, time_taps, height_taps, tf_hbm, ti_hbm, hf_hbm, hi_hbm,
    out,
    frames, tf, ti, hf, hi, t_response, h_response,
    t_send, t_have, t_done, t_back, h_send, h_have, h_done, h_back,
    load_sems, send_sems, recv_sems,
):
    frames_dev, rows_dev, lane_total = frames.shape
    width = lane_total // CHUNKS
    groups = width // LANE
    block = frames_dev * rows_dev
    tm = lax.axis_index("tm")
    height = lax.axis_index("height")
    row_size = 4
    y_count = height_count // row_size

    loads = [
        pltpu.make_async_copy(src, dst, load_sems.at[i])
        for i, (src, dst) in enumerate(
            [
                (frames_hbm, frames), (tf_hbm, tf), (ti_hbm, ti), (hf_hbm, hf), (hi_hbm, hi),
                (frames_hbm.at[:, :, pl.ds(width, width)], h_send.at[1]),
            ]
        )
    ]
    for load in loads:
        load.start()

    barrier = pltpu.get_barrier_semaphore()

    def tm_peer(d):
        return lax.rem(tm + d, tm_count)

    def height_peer(i):
        k = lax.rem(lax.div(i, 2), y_count)
        away = y_count // 2 + lax.div(k + 1, 2) * (1 - 2 * lax.rem(k, 2))
        cross = lax.rem(lax.div(height, 2) + 1 - lax.div(i, 2 * y_count), 2)
        core = lax.rem(height + 1 - lax.rem(i, 2), 2)
        return lax.rem(lax.div(height, row_size) + away, y_count) * row_size + cross * 2 + core

    def each_tm(act):
        act(tm_peer(tm_count // 2))

        def pair(m, carry):
            act(tm_peer(tm_count // 2 - m))
            act(tm_peer(tm_count // 2 + m))
            return carry

        lax.fori_loop(1, tm_count // 2, pair, 0)

    def each_height(act):
        def one(i, carry):
            act(height_peer(i))
            return carry

        lax.fori_loop(0, height_count - 1, one, 0)

    each_tm(lambda peer: pl.semaphore_signal(barrier, inc=1, device_id=(peer, height), device_id_type=MESH))
    each_height(lambda peer: pl.semaphore_signal(barrier, inc=1, device_id=(tm, peer), device_id_type=MESH))

    loads[0].wait()
    swap_in = one_hot((block, block), lambda r, c: c == (r % frames_dev) * rows_dev + r // frames_dev)
    swap_back = one_hot((block, block), lambda r, c: c == (r % rows_dev) * frames_dev + r // rows_dev)

    def rows_first(values, c):
        flat = values.astype(F32).reshape(block, width).astype(BF16)
        turned = dot(swap_in, flat).astype(BF16)
        for g in range(groups):
            t_send[c, g * rows_dev:(g + 1) * rows_dev] = turned[:, g * LANE:(g + 1) * LANE].reshape(
                rows_dev, frames_dev, LANE
            )

    def frames_first(c, g):
        tile = t_back[c, g * rows_dev:(g + 1) * rows_dev].reshape(block, LANE)
        return dot(swap_back, tile).reshape(frames_dev, rows_dev, LANE)

    rows_first(frames[:, :, :width], 0)
    loads[5].wait()

    pl.semaphore_wait(barrier, tm_count + height_count - 2)

    def exchange_tm(phase, c, src, dst):
        each_tm(lambda peer: pltpu.make_async_remote_copy(
            src_ref=src.at[c, peer], dst_ref=dst.at[c, tm],
            send_sem=send_sems.at[phase, c], recv_sem=recv_sems.at[phase, c],
            device_id=(peer, height), device_id_type=MESH,
        ).start())
        pltpu.make_async_copy(src.at[c, tm], dst.at[c, tm], recv_sems.at[phase, c]).start()

    def exchange_height(phase, c, src, dst):
        each_height(lambda peer: pltpu.make_async_remote_copy(
            src_ref=src.at[c, peer], dst_ref=dst.at[c, height],
            send_sem=send_sems.at[phase, c], recv_sem=recv_sems.at[phase, c],
            device_id=(tm, peer), device_id_type=MESH,
        ).start())
        pltpu.make_async_copy(src.at[c, height], dst.at[c, height], recv_sems.at[phase, c]).start()

    def arrived(phase, c, dst):
        pltpu.make_async_copy(dst.at[c], dst.at[c], recv_sems.at[phase, c]).wait()

    def departed(phase, c, src, peers):
        sent = src.at[c, pl.ds(0, peers - 1)]
        pltpu.make_async_copy(sent, sent, send_sems.at[phase, c]).wait()

    def time_stage(c):
        arrived(0, c, t_have)
        values = t_have[c].reshape(tm_count * frames_dev, LANE)
        result = time_inverse(ti, *product(t_response, *time_forward(tf, values))).astype(BF16)
        t_done[c] = result.reshape(tm_count, frames_dev, LANE)
        exchange_tm(1, c, t_done, t_back)

    def height_stage(c):
        arrived(2, c, h_have)
        values = h_have[c].astype(F32).reshape(height_count * rows_dev, width).astype(BF16)
        result = height_inverse(hi, *product(h_response, *height_forward(hf, values)))
        h_done[c] = result.reshape(height_count, rows_dev, width).astype(BF16)
        exchange_height(3, c, h_done, h_back)

    exchange_height(2, 1, h_send, h_have)
    exchange_tm(0, 0, t_send, t_have)
    for load in loads[1:5]:
        load.wait()
    store_response(height_forward, hf, height_taps, h_response)
    store_response(time_forward, tf, time_taps, t_response)

    height_stage(1)
    time_stage(0)

    arrived(3, 1, h_back)
    rows_first(h_back[1], 1)
    exchange_tm(0, 1, t_send, t_have)

    arrived(1, 0, t_back)
    for g in range(groups):
        h_send[0, :, :, g * LANE:(g + 1) * LANE] = frames_first(0, g).astype(BF16)
    exchange_height(2, 0, h_send, h_have)

    time_stage(1)
    height_stage(0)

    arrived(3, 0, h_back)
    out[:, :, :width] = (frames[:, :, :width].astype(F32) + h_back[0].astype(F32)).astype(BF16)

    arrived(1, 1, t_back)
    for g in range(groups):
        lanes = slice(width + g * LANE, width + (g + 1) * LANE)
        out[:, :, lanes] = (frames[:, :, lanes].astype(F32) + frames_first(1, g)).astype(BF16)

    for c in range(CHUNKS):
        departed(0, c, t_send, tm_count)
        departed(1, c, t_done, tm_count)
        departed(2, c, h_send, height_count)
        departed(3, c, h_done, height_count)


def shards(frames_in, time_filter, height_filter):
    frames_dev, rows_dev, lane_total = frames_in.shape
    tm_count = lax.axis_size("tm")
    height_count = lax.axis_size("height")
    width = lane_total // CHUNKS
    tf, ti = time_tables(time_filter.shape[0])
    hf, hi = height_tables(height_filter.shape[0])
    t_buf = pltpu.VMEM((CHUNKS, tm_count, frames_dev, LANE), BF16)
    h_buf = pltpu.VMEM((CHUNKS, height_count, rows_dev, width), BF16)
    like = lambda a: pltpu.VMEM(a.shape, BF16)
    hbm = pl.BlockSpec(memory_space=pl.ANY)
    vmem = pl.BlockSpec(memory_space=pltpu.VMEM)
    return pl.pallas_call(
        functools.partial(kernel, tm_count, height_count),
        out_shape=jax.ShapeDtypeStruct(frames_in.shape, BF16),
        in_specs=[hbm, vmem, vmem, hbm, hbm, hbm, hbm],
        out_specs=vmem,
        scratch_shapes=[
            pltpu.VMEM(frames_in.shape, BF16),
            like(tf), like(ti), like(hf), like(hi),
            pltpu.VMEM((3, time_filter.shape[0] // 2, LANE), F32),
            pltpu.VMEM((3, height_filter.shape[0] // 2, LANE), F32),
            t_buf, t_buf, t_buf, t_buf, h_buf, h_buf, h_buf, h_buf,
            pltpu.SemaphoreType.DMA((6,)),
            pltpu.SemaphoreType.DMA((4, CHUNKS)),
            pltpu.SemaphoreType.DMA((4, CHUNKS)),
        ],
        compiler_params=pltpu.CompilerParams(collective_id=0, has_side_effects=True),
    )(frames_in, time_filter.T, height_filter.T, jnp.asarray(tf), jnp.asarray(ti), jnp.asarray(hf), jnp.asarray(hi))


def solution(mesh):
    return jax.shard_map(
        shards,
        mesh=mesh,
        in_specs=(P("tm", "height", None), P(), P()),
        out_specs=P("tm", "height", None),
        check_vma=False,
    )
```

```python
import functools

import jax
import jax.numpy as jnp
import numpy as np
from jax import lax
from jax.experimental import pallas as pl
from jax.experimental.pallas import tpu as pltpu
from jax.sharding import PartitionSpec as P

MESH = pl.DeviceIdType.MESH
F32, BF16 = jnp.float32, jnp.bfloat16
LANE = 128
CHUNKS = 2


def split(table):
    high = table.astype(np.float32).astype(jnp.bfloat16)
    low = (table - high.astype(np.float64)).astype(np.float32).astype(jnp.bfloat16)
    return high, low


def dft_rows(size):
    half = size // 2
    order = np.concatenate([np.arange(0, half, 2), np.arange(1, half, 2)])
    angle = 2.0 * np.pi * ((order[:, None] * np.arange(size)[None, :]) % size) / size
    sines = np.sin(angle)
    sines[0] = np.cos(np.pi * np.arange(size))
    return np.cos(angle), sines


def time_tables(size):
    half, quarter = size // 2, size // 4
    cosines, sines = dft_rows(size)
    parts = [
        np.concatenate([cosines[rows, :half], sines[rows, :half]], axis=0)
        for rows in (slice(0, quarter), slice(quarter, half))
    ]
    forward = np.concatenate(split(np.concatenate(parts, axis=0)), axis=0)
    inverse = np.stack([piece for part in parts for piece in split(part.T)])
    return forward, inverse


def height_tables(size):
    high, low = split(np.concatenate(dft_rows(size), axis=0))
    return np.concatenate([high, low], axis=1), np.concatenate([high.T, low.T], axis=1)


def dot(a, b):
    return jnp.dot(a, b, preferred_element_type=F32)


def halves(values):
    high = values.astype(BF16)
    return high, (values - high.astype(F32)).astype(BF16)


def one_hot(shape, hit):
    rows = lax.broadcasted_iota(jnp.int32, shape, 0)
    cols = lax.broadcasted_iota(jnp.int32, shape, 1)
    return jnp.where(hit(rows, cols), 1.0, 0.0).astype(BF16)


def time_forward(table, values):
    half, quarter = values.shape[0] // 2, values.shape[0] // 4
    both = dot(table[...], jnp.concatenate([values[:half], values[half:]], axis=1))
    both = both[:2 * half] + both[2 * half:]
    even = both[:half, :LANE] + both[:half, LANE:]
    odd = both[half:, :LANE] - both[half:, LANE:]
    cosine = jnp.concatenate([even[:quarter], odd[:quarter]], axis=0)
    sine = jnp.concatenate([even[quarter:], odd[quarter:]], axis=0)
    return cosine, sine


def time_inverse(table, cosine, sine):
    quarter = cosine.shape[0] // 2
    sums = []
    for p in range(2):
        rows = slice(p * quarter, (p + 1) * quarter)
        high, low = halves(jnp.concatenate([cosine[rows], sine[rows]], axis=0))
        main = dot(table[2 * p], jnp.concatenate([high, low], axis=1))
        sums.append(main[:, :LANE] + main[:, LANE:] + dot(table[2 * p + 1], high))
    return jnp.concatenate([sums[0] + sums[1], sums[0] - sums[1]], axis=0)


def height_forward(table, values):
    half = values.shape[0] // 2
    both = dot(table[...], jnp.concatenate([values, values], axis=0))
    return both[:half], both[half:]


def height_inverse(table, cosine, sine):
    high, low = halves(jnp.concatenate([cosine, sine], axis=0))
    return dot(table[...], jnp.concatenate([high, high], axis=0)) + dot(table[:, :high.shape[0]], low)


def store_response(forward, table, taps, response):
    channels, size = taps.shape
    spread = one_hot((LANE, channels), lambda r, c: c == r % channels)
    wide = jnp.transpose(dot(spread, taps[...])).astype(BF16)
    cosine, sine = forward(table, wide)
    first = lax.broadcasted_iota(jnp.int32, cosine.shape, 0) == 0
    scale = jnp.where(first, 1.0 / size, 2.0 / size)
    cosine, sine = cosine * scale, sine * scale
    response[0] = cosine
    response[1] = jnp.where(first, 0.0, sine)
    response[2] = jnp.where(first, sine, cosine)


def product(response, cosine, sine):
    wide = lambda which: jnp.concatenate([response[which]] * (cosine.shape[1] // LANE), axis=1)
    p, q, nyquist_p = wide(0), wide(1), wide(2)
    return cosine * p - sine * q, cosine * q + sine * nyquist_p


def kernel(
    tm_count, height_count,
    frames_hbm, tt_hbm, ht_hbm, tf_hbm, ti_hbm, hf_hbm, hi_hbm,
    out,
    frames, time_taps, height_taps, tf, ti, hf, hi, t_response, h_response,
    t_send, t_have, t_done, t_back, h_send, h_have, h_done, h_back,
    load_sems, send_sems, recv_sems,
):
    frames_dev, rows_dev, lane_total = frames.shape
    width = lane_total // CHUNKS
    groups = width // LANE
    block = frames_dev * rows_dev
    tm = lax.axis_index("tm")
    height = lax.axis_index("height")

    barrier = pltpu.get_barrier_semaphore()

    def tm_peer(d):
        return lax.rem(tm + d, tm_count)

    row, column, core = lax.div(height, 4), lax.rem(lax.div(height, 2), 2), lax.rem(height, 2)
    y_count = height_count // 4
    rows_at = [lax.rem(row + away, y_count) * 4 for away in range(y_count)]
    pairs_at = [(lax.rem(column + x, 2)) * 2 + lax.rem(core + c, 2) for x in (1, 0) for c in (1, 0)]
    by_hops = sorted(range(y_count), key=lambda away: -min(away, y_count - away))
    height_peers = [rows_at[y] + pairs_at[2 * x + c] for x in (0, 1) for y in by_hops for c in (0, 1)][:-1]

    def each_tm(act):
        act(tm_peer(tm_count // 2))

        def pair(m, carry):
            act(tm_peer(tm_count // 2 - m))
            act(tm_peer(tm_count // 2 + m))
            return carry

        lax.fori_loop(1, tm_count // 2, pair, 0)

    def each_height(act):
        for peer in height_peers:
            act(peer)

    each_tm(lambda peer: pl.semaphore_signal(barrier, inc=1, device_id=(peer, height), device_id_type=MESH))
    each_height(lambda peer: pl.semaphore_signal(barrier, inc=1, device_id=(tm, peer), device_id_type=MESH))

    loads = [
        pltpu.make_async_copy(src, dst, load_sems.at[i])
        for i, (src, dst) in enumerate([
            (frames_hbm, frames), (frames_hbm.at[:, :, pl.ds(width, width)], h_send.at[1]),
            (ht_hbm, height_taps), (hf_hbm, hf), (tt_hbm, time_taps), (tf_hbm, tf), (hi_hbm, hi), (ti_hbm, ti),
        ])
    ]
    for load in loads:
        load.start()

    loads[0].wait()
    swap_in = one_hot((block, block), lambda r, c: c == (r % frames_dev) * rows_dev + r // frames_dev)
    swap_back = one_hot((block, block), lambda r, c: c == (r % rows_dev) * frames_dev + r // rows_dev)

    def rows_first(values, c):
        flat = values.astype(F32).reshape(block, width).astype(BF16)
        turned = dot(swap_in, flat).astype(BF16)
        for g in range(groups):
            t_send[c, g * rows_dev:(g + 1) * rows_dev] = turned[:, g * LANE:(g + 1) * LANE].reshape(
                rows_dev, frames_dev, LANE
            )

    def frames_first(c, g):
        tile = t_back[c, g * rows_dev:(g + 1) * rows_dev].reshape(block, LANE)
        return dot(swap_back, tile).reshape(frames_dev, rows_dev, LANE)

    rows_first(frames[:, :, :width], 0)
    loads[1].wait()

    pl.semaphore_wait(barrier, tm_count + height_count - 2)

    def exchange_tm(phase, c, src, dst):
        each_tm(lambda peer: pltpu.make_async_remote_copy(
            src_ref=src.at[c, peer], dst_ref=dst.at[c, tm],
            send_sem=send_sems.at[phase, c], recv_sem=recv_sems.at[phase, c],
            device_id=(peer, height), device_id_type=MESH,
        ).start())
        pltpu.make_async_copy(src.at[c, tm], dst.at[c, tm], recv_sems.at[phase, c]).start()

    def exchange_height(phase, c, src, dst):
        each_height(lambda peer: pltpu.make_async_remote_copy(
            src_ref=src.at[c, peer], dst_ref=dst.at[c, height],
            send_sem=send_sems.at[phase, c], recv_sem=recv_sems.at[phase, c],
            device_id=(tm, peer), device_id_type=MESH,
        ).start())
        pltpu.make_async_copy(src.at[c, height], dst.at[c, height], recv_sems.at[phase, c]).start()

    def arrived(phase, c, dst):
        pltpu.make_async_copy(dst.at[c], dst.at[c], recv_sems.at[phase, c]).wait()

    def departed(phase, c, src, peers):
        sent = src.at[c, pl.ds(0, peers - 1)]
        pltpu.make_async_copy(sent, sent, send_sems.at[phase, c]).wait()

    def time_stage(c):
        arrived(0, c, t_have)
        values = t_have[c].reshape(tm_count * frames_dev, LANE)
        result = time_inverse(ti, *product(t_response, *time_forward(tf, values))).astype(BF16)
        t_done[c] = result.reshape(tm_count, frames_dev, LANE)
        exchange_tm(1, c, t_done, t_back)

    def height_stage(c):
        arrived(2, c, h_have)
        values = h_have[c].astype(F32).reshape(height_count * rows_dev, width).astype(BF16)
        result = height_inverse(hi, *product(h_response, *height_forward(hf, values)))
        h_done[c] = result.reshape(height_count, rows_dev, width).astype(BF16)
        exchange_height(3, c, h_done, h_back)

    exchange_height(2, 1, h_send, h_have)
    exchange_tm(0, 0, t_send, t_have)
    for load in loads[2:]:
        load.wait()
    store_response(height_forward, hf, height_taps, h_response)
    store_response(time_forward, tf, time_taps, t_response)

    height_stage(1)
    time_stage(0)

    arrived(3, 1, h_back)
    rows_first(h_back[1], 1)
    exchange_tm(0, 1, t_send, t_have)

    arrived(1, 0, t_back)
    for g in range(groups):
        h_send[0, :, :, g * LANE:(g + 1) * LANE] = frames_first(0, g).astype(BF16)
    exchange_height(2, 0, h_send, h_have)

    time_stage(1)
    height_stage(0)

    arrived(3, 0, h_back)
    out[:, :, :width] = (frames[:, :, :width].astype(F32) + h_back[0].astype(F32)).astype(BF16)

    arrived(1, 1, t_back)
    for g in range(groups):
        lanes = slice(width + g * LANE, width + (g + 1) * LANE)
        out[:, :, lanes] = (frames[:, :, lanes].astype(F32) + frames_first(1, g)).astype(BF16)

    for c in range(CHUNKS):
        departed(0, c, t_send, tm_count)
        departed(1, c, t_done, tm_count)
        departed(2, c, h_send, height_count)
        departed(3, c, h_done, height_count)


def shards(frames_in, time_filter, height_filter):
    frames_dev, rows_dev, lane_total = frames_in.shape
    tm_count = lax.axis_size("tm")
    height_count = lax.axis_size("height")
    width = lane_total // CHUNKS
    tf, ti = time_tables(time_filter.shape[0])
    hf, hi = height_tables(height_filter.shape[0])
    t_buf = pltpu.VMEM((CHUNKS, tm_count, frames_dev, LANE), BF16)
    h_buf = pltpu.VMEM((CHUNKS, height_count, rows_dev, width), BF16)
    like = lambda a: pltpu.VMEM(a.shape, BF16)
    hbm = pl.BlockSpec(memory_space=pltpu.MemorySpace.HBM)
    vmem = pl.BlockSpec(memory_space=pltpu.VMEM)
    return pl.pallas_call(
        functools.partial(kernel, tm_count, height_count),
        out_shape=pltpu.VMEM(frames_in.shape, BF16),
        in_specs=[hbm] * 7,
        out_specs=vmem,
        scratch_shapes=[
            pltpu.VMEM(frames_in.shape, BF16),
            like(time_filter.T), like(height_filter.T), like(tf), like(ti), like(hf), like(hi),
            pltpu.VMEM((3, time_filter.shape[0] // 2, LANE), F32),
            pltpu.VMEM((3, height_filter.shape[0] // 2, LANE), F32),
            t_buf, t_buf, t_buf, t_buf, h_buf, h_buf, h_buf, h_buf,
            pltpu.SemaphoreType.DMA((8,)),
            pltpu.SemaphoreType.DMA((4, CHUNKS)),
            pltpu.SemaphoreType.DMA((4, CHUNKS)),
        ],
        compiler_params=pltpu.CompilerParams(collective_id=0, has_side_effects=True),
    )(frames_in, time_filter.T, height_filter.T, jnp.asarray(tf), jnp.asarray(ti), jnp.asarray(hf), jnp.asarray(hi))


def solution(mesh):
    return jax.shard_map(
        shards,
        mesh=mesh,
        in_specs=(P("tm", "height", None), P(), P()),
        out_specs=P("tm", "height", None),
        check_vma=False,
    )
```

```python
import functools

import jax
import jax.numpy as jnp
import numpy as np
from jax import lax
from jax.experimental import pallas as pl
from jax.experimental.pallas import tpu as pltpu
from jax.sharding import PartitionSpec as P

MESH = pl.DeviceIdType.MESH
F32, BF16 = jnp.float32, jnp.bfloat16
LANE = 128
CHUNKS = 2
EARLY_PLANES = 8


def split(table):
    high = table.astype(np.float32).astype(jnp.bfloat16)
    low = (table - high.astype(np.float64)).astype(np.float32).astype(jnp.bfloat16)
    return high, low


def dft_rows(size):
    half = size // 2
    order = np.concatenate([np.arange(0, half, 2), np.arange(1, half, 2)])
    angle = 2.0 * np.pi * ((order[:, None] * np.arange(size)[None, :]) % size) / size
    sines = np.sin(angle)
    sines[0] = np.cos(np.pi * np.arange(size))
    return np.cos(angle), sines


def time_tables(size):
    half, quarter = size // 2, size // 4
    cosines, sines = dft_rows(size)
    parts = [
        np.concatenate([cosines[rows, :half], sines[rows, :half]], axis=0)
        for rows in (slice(0, quarter), slice(quarter, half))
    ]
    forward = np.concatenate(split(np.concatenate(parts, axis=0)), axis=1)
    inverse = np.stack([piece for part in parts for piece in split(part.T)])
    return forward, inverse


def height_tables(size):
    high, low = split(np.concatenate(dft_rows(size), axis=0))
    return np.concatenate([high, low], axis=1), np.concatenate([high.T, low.T], axis=1)


def dot(a, b):
    return jnp.dot(a, b, preferred_element_type=F32)


def halves(values):
    high = values.astype(BF16)
    return high, (values - high.astype(F32)).astype(BF16)


def one_hot(shape, hit):
    rows = lax.broadcasted_iota(jnp.int32, shape, 0)
    cols = lax.broadcasted_iota(jnp.int32, shape, 1)
    return jnp.where(hit(rows, cols), 1.0, 0.0).astype(BF16)


def time_forward(table, values):
    half, quarter = values.shape[0] // 2, values.shape[0] // 4
    pair = jnp.concatenate([values[:half], values[half:]], axis=1)
    both = dot(table[...], jnp.concatenate([pair, pair], axis=0))
    even = both[:half, :LANE] + both[:half, LANE:]
    odd = both[half:, :LANE] - both[half:, LANE:]
    cosine = jnp.concatenate([even[:quarter], odd[:quarter]], axis=0)
    sine = jnp.concatenate([even[quarter:], odd[quarter:]], axis=0)
    return cosine, sine


def time_inverse(table, cosine, sine):
    quarter = cosine.shape[0] // 2
    sums = []
    for p in range(2):
        rows = slice(p * quarter, (p + 1) * quarter)
        high, low = halves(jnp.concatenate([cosine[rows], sine[rows]], axis=0))
        main = dot(table[2 * p], jnp.concatenate([high, low], axis=1))
        sums.append(main[:, :LANE] + main[:, LANE:] + dot(table[2 * p + 1], high))
    return jnp.concatenate([sums[0] + sums[1], sums[0] - sums[1]], axis=0)


def height_forward(table, values):
    half = values.shape[0] // 2
    both = dot(table[...], jnp.concatenate([values, values], axis=0))
    return both[:half], both[half:]


def height_inverse(table, cosine, sine):
    high, low = halves(jnp.concatenate([cosine, sine], axis=0))
    return dot(table[...], jnp.concatenate([high, high], axis=0)) + dot(table[:, :high.shape[0]], low)


def store_response(forward, table, taps, response):
    channels, size = taps.shape
    spread = one_hot((LANE, channels), lambda r, c: c == r % channels)
    wide = jnp.transpose(dot(spread, taps[...])).astype(BF16)
    cosine, sine = forward(table, wide)
    first = lax.broadcasted_iota(jnp.int32, cosine.shape, 0) == 0
    scale = jnp.where(first, 1.0 / size, 2.0 / size)
    cosine, sine = cosine * scale, sine * scale
    response[0] = cosine
    response[1] = jnp.where(first, 0.0, sine)
    response[2] = jnp.where(first, sine, cosine)


def product(response, cosine, sine):
    wide = lambda which: jnp.concatenate([response[which]] * (cosine.shape[1] // LANE), axis=1)
    p, q, nyquist_p = wide(0), wide(1), wide(2)
    return cosine * p - sine * q, cosine * q + sine * nyquist_p


def kernel(
    tm_count, height_count,
    frames_hbm, tt_hbm, ht_hbm, tf_hbm, ti_hbm, hf_hbm, hi_hbm,
    out,
    frames, time_taps, height_taps, tf, ti, hf, hi, t_response, h_response,
    t_send, t_have, t_done, t_back, h_send, h_have, h_done, h_back,
    load_sems, send_sems, recv_sems,
):
    frames_dev, rows_dev, lane_total = frames.shape
    width = lane_total // CHUNKS
    groups = width // LANE
    block = frames_dev * rows_dev
    tm = lax.axis_index("tm")
    height = lax.axis_index("height")

    barrier = pltpu.get_barrier_semaphore()

    def tm_peer(d):
        return lax.rem(tm + d, tm_count)

    row, column, core = lax.div(height, 4), lax.rem(lax.div(height, 2), 2), lax.rem(height, 2)
    y_count = height_count // 4
    rows_at = [lax.rem(row + away, y_count) * 4 for away in range(y_count)]
    pairs_at = [(lax.rem(column + x, 2)) * 2 + lax.rem(core + c, 2) for x in (1, 0) for c in (1, 0)]
    by_hops = sorted(range(y_count), key=lambda away: -min(away, y_count - away))
    height_peers = [rows_at[y] + pairs_at[2 * x + c] for x in (0, 1) for y in by_hops for c in (0, 1)][:-1]

    def each_tm(act):
        act(tm_peer(tm_count // 2))

        def pair(m, carry):
            act(tm_peer(tm_count // 2 - m))
            act(tm_peer(tm_count // 2 + m))
            return carry

        lax.fori_loop(1, tm_count // 2, pair, 0)

    def each_height(act):
        for peer in height_peers:
            act(peer)

    each_tm(lambda peer: pl.semaphore_signal(barrier, inc=1, device_id=(peer, height), device_id_type=MESH))
    each_height(lambda peer: pl.semaphore_signal(barrier, inc=1, device_id=(tm, peer), device_id_type=MESH))

    loads = [
        pltpu.make_async_copy(src, dst, load_sems.at[i])
        for i, (src, dst) in enumerate([
            (frames_hbm, frames), (frames_hbm.at[:, :, pl.ds(width, width)], h_send.at[1]),
            (ht_hbm, height_taps), (hf_hbm, hf), (tt_hbm, time_taps), (tf_hbm, tf), (hi_hbm, hi), (ti_hbm, ti),
        ])
    ]
    for load in loads:
        load.start()

    loads[0].wait()
    swap_in = one_hot((block, block), lambda r, c: c == (r % frames_dev) * rows_dev + r // frames_dev)
    swap_back = one_hot((block, block), lambda r, c: c == (r % rows_dev) * frames_dev + r // rows_dev)

    def rows_first(values, c):
        flat = values.astype(F32).reshape(block, width).astype(BF16)
        turned = dot(swap_in, flat).astype(BF16)
        for g in range(groups):
            t_send[c, g * rows_dev:(g + 1) * rows_dev] = turned[:, g * LANE:(g + 1) * LANE].reshape(
                rows_dev, frames_dev, LANE
            )

    def frames_first(c, g):
        tile = t_back[c, g * rows_dev:(g + 1) * rows_dev].reshape(block, LANE)
        return dot(swap_back, tile).reshape(frames_dev, rows_dev, LANE)

    rows_first(frames[:, :, :width], 0)
    loads[1].wait()

    pl.semaphore_wait(barrier, tm_count + height_count - 2)

    def exchange_tm(phase, c, src, dst):
        each_tm(lambda peer: pltpu.make_async_remote_copy(
            src_ref=src.at[c, peer], dst_ref=dst.at[c, tm],
            send_sem=send_sems.at[phase, c], recv_sem=recv_sems.at[phase, c],
            device_id=(peer, height), device_id_type=MESH,
        ).start())
        pltpu.make_async_copy(src.at[c, tm], dst.at[c, tm], recv_sems.at[phase, c]).start()

    def from_home(c, first, last):
        def send(peer, carry):
            @pl.when(peer != tm)
            def _():
                pltpu.make_async_remote_copy(
                    src_ref=t_done.at[c, peer], dst_ref=t_back.at[c, tm],
                    send_sem=send_sems.at[1, c], recv_sem=recv_sems.at[1, c],
                    device_id=(peer, height), device_id_type=MESH,
                ).start()

            return carry

        lax.fori_loop(first, last, send, 0)

    def own_frames(c):
        pltpu.make_async_copy(t_done.at[c, tm], t_back.at[c, tm], recv_sems.at[1, c]).start()

    def exchange_height(phase, c, src, dst):
        each_height(lambda peer: pltpu.make_async_remote_copy(
            src_ref=src.at[c, peer], dst_ref=dst.at[c, height],
            send_sem=send_sems.at[phase, c], recv_sem=recv_sems.at[phase, c],
            device_id=(tm, peer), device_id_type=MESH,
        ).start())
        pltpu.make_async_copy(src.at[c, height], dst.at[c, height], recv_sems.at[phase, c]).start()

    def arrived(phase, c, dst):
        pltpu.make_async_copy(dst.at[c], dst.at[c], recv_sems.at[phase, c]).wait()

    def departed(phase, c, src, peers):
        sent = src.at[c, pl.ds(0, peers - 1)]
        pltpu.make_async_copy(sent, sent, send_sems.at[phase, c]).wait()

    def time_stage(c):
        arrived(0, c, t_have)
        values = t_have[c].reshape(tm_count * frames_dev, LANE)
        result = time_inverse(ti, *product(t_response, *time_forward(tf, values))).astype(BF16)
        t_done[c] = result.reshape(tm_count, frames_dev, LANE)
        own_frames(c)

    def height_stage(c):
        arrived(2, c, h_have)
        values = h_have[c].astype(F32).reshape(height_count * rows_dev, width).astype(BF16)
        result = height_inverse(hi, *product(h_response, *height_forward(hf, values)))
        h_done[c] = result.reshape(height_count, rows_dev, width).astype(BF16)
        exchange_height(3, c, h_done, h_back)

    exchange_height(2, 1, h_send, h_have)
    exchange_tm(0, 0, t_send, t_have)
    for load in loads[2:]:
        load.wait()
    store_response(height_forward, hf, height_taps, h_response)
    store_response(time_forward, tf, time_taps, t_response)

    early = EARLY_PLANES * 2

    def turn_to_height():
        arrived(1, 0, t_back)
        for g in range(groups):
            h_send[0, :, :, g * LANE:(g + 1) * LANE] = frames_first(0, g).astype(BF16)
        exchange_height(2, 0, h_send, h_have)

    height_stage(1)
    time_stage(0)
    from_home(0, 0, early)

    arrived(3, 1, h_back)
    rows_first(h_back[1], 1)
    exchange_tm(0, 1, t_send, t_have)
    from_home(0, early, tm_count)

    @pl.when(tm < early)
    def _():
        turn_to_height()

    time_stage(1)
    from_home(1, 0, tm_count)

    @pl.when(tm >= early)
    def _():
        turn_to_height()

    height_stage(0)

    arrived(3, 0, h_back)
    out[:, :, :width] = (frames[:, :, :width].astype(F32) + h_back[0].astype(F32)).astype(BF16)

    arrived(1, 1, t_back)
    for g in range(groups):
        lanes = slice(width + g * LANE, width + (g + 1) * LANE)
        out[:, :, lanes] = (frames[:, :, lanes].astype(F32) + frames_first(1, g)).astype(BF16)

    for c in range(CHUNKS):
        departed(0, c, t_send, tm_count)
        departed(1, c, t_done, tm_count)
        departed(2, c, h_send, height_count)
        departed(3, c, h_done, height_count)


def shards(frames_in, time_filter, height_filter):
    frames_dev, rows_dev, lane_total = frames_in.shape
    tm_count = lax.axis_size("tm")
    height_count = lax.axis_size("height")
    width = lane_total // CHUNKS
    tf, ti = time_tables(time_filter.shape[0])
    hf, hi = height_tables(height_filter.shape[0])
    t_buf = pltpu.VMEM((CHUNKS, tm_count, frames_dev, LANE), BF16)
    h_buf = pltpu.VMEM((CHUNKS, height_count, rows_dev, width), BF16)
    like = lambda a: pltpu.VMEM(a.shape, BF16)
    hbm = pl.BlockSpec(memory_space=pltpu.MemorySpace.HBM)
    vmem = pl.BlockSpec(memory_space=pltpu.VMEM)
    return pl.pallas_call(
        functools.partial(kernel, tm_count, height_count),
        out_shape=pltpu.VMEM(frames_in.shape, BF16),
        in_specs=[hbm] * 7,
        out_specs=vmem,
        scratch_shapes=[
            pltpu.VMEM(frames_in.shape, BF16),
            like(time_filter.T), like(height_filter.T), like(tf), like(ti), like(hf), like(hi),
            pltpu.VMEM((3, time_filter.shape[0] // 2, LANE), F32),
            pltpu.VMEM((3, height_filter.shape[0] // 2, LANE), F32),
            t_buf, t_buf, t_buf, t_buf, h_buf, h_buf, h_buf, h_buf,
            pltpu.SemaphoreType.DMA((8,)),
            pltpu.SemaphoreType.DMA((4, CHUNKS)),
            pltpu.SemaphoreType.DMA((4, CHUNKS)),
        ],
        compiler_params=pltpu.CompilerParams(collective_id=0, has_side_effects=True),
    )(frames_in, time_filter.T, height_filter.T, jnp.asarray(tf), jnp.asarray(ti), jnp.asarray(hf), jnp.asarray(hi))


def solution(mesh):
    return jax.shard_map(
        shards,
        mesh=mesh,
        in_specs=(P("tm", "height", None), P(), P()),
        out_specs=P("tm", "height", None),
        check_vma=False,
    )
```

```python
import functools

import jax
import jax.numpy as jnp
import numpy as np
from jax import lax
from jax.experimental import pallas as pl
from jax.experimental.pallas import tpu as pltpu
from jax.sharding import PartitionSpec as P

MESH = pl.DeviceIdType.MESH
F32, BF16 = jnp.float32, jnp.bfloat16
LANE = 128
CHUNKS = 2
EARLY_PLANES = 8


def split(table):
    high = table.astype(np.float32).astype(jnp.bfloat16)
    low = (table - high.astype(np.float64)).astype(np.float32).astype(jnp.bfloat16)
    return high, low


def dft_rows(size):
    half = size // 2
    order = np.concatenate([np.arange(0, half, 2), np.arange(1, half, 2)])
    angle = 2.0 * np.pi * ((order[:, None] * np.arange(size)[None, :]) % size) / size
    sines = np.sin(angle)
    sines[0] = np.cos(np.pi * np.arange(size))
    return np.cos(angle), sines


def time_tables(size):
    half, quarter = size // 2, size // 4
    cosines, sines = dft_rows(size)
    parts = [
        np.concatenate([cosines[rows, :half], sines[rows, :half]], axis=0)
        for rows in (slice(0, quarter), slice(quarter, half))
    ]
    forward = np.concatenate(split(np.concatenate(parts, axis=0)), axis=1)
    inverse = np.stack([piece for part in parts for piece in split(part.T)])
    return forward, inverse


def height_tables(size):
    high, low = split(np.concatenate(dft_rows(size), axis=0))
    return np.concatenate([high, low], axis=1), np.concatenate([high.T, low.T], axis=1)


def dot(a, b):
    return jnp.dot(a, b, preferred_element_type=F32)


def halves(values):
    high = values.astype(BF16)
    return high, (values - high.astype(F32)).astype(BF16)


def one_hot(shape, hit):
    rows = lax.broadcasted_iota(jnp.int32, shape, 0)
    cols = lax.broadcasted_iota(jnp.int32, shape, 1)
    return jnp.where(hit(rows, cols), 1.0, 0.0).astype(BF16)


def time_forward(table, values):
    half, quarter = values.shape[0] // 2, values.shape[0] // 4
    pair = jnp.concatenate([values[:half], values[half:]], axis=1)
    both = dot(table[...], jnp.concatenate([pair, pair], axis=0))
    even = both[:half, :LANE] + both[:half, LANE:]
    odd = both[half:, :LANE] - both[half:, LANE:]
    cosine = jnp.concatenate([even[:quarter], odd[:quarter]], axis=0)
    sine = jnp.concatenate([even[quarter:], odd[quarter:]], axis=0)
    return cosine, sine


def time_inverse(table, cosine, sine):
    quarter = cosine.shape[0] // 2
    sums = []
    for p in range(2):
        rows = slice(p * quarter, (p + 1) * quarter)
        high, low = halves(jnp.concatenate([cosine[rows], sine[rows]], axis=0))
        main = dot(table[2 * p], jnp.concatenate([high, low], axis=1))
        sums.append(main[:, :LANE] + main[:, LANE:] + dot(table[2 * p + 1], high))
    return jnp.concatenate([sums[0] + sums[1], sums[0] - sums[1]], axis=0)


def height_forward(table, values):
    half = values.shape[0] // 2
    both = dot(table[...], jnp.concatenate([values, values], axis=0))
    return both[:half], both[half:]


def height_inverse(table, cosine, sine):
    high, low = halves(jnp.concatenate([cosine, sine], axis=0))
    return dot(table[...], jnp.concatenate([high, high], axis=0)) + dot(table[:, :high.shape[0]], low)


def store_response(forward, table, taps, response):
    channels, size = taps.shape
    spread = one_hot((LANE, channels), lambda r, c: c == r % channels)
    wide = jnp.transpose(dot(spread, taps[...])).astype(BF16)
    cosine, sine = forward(table, wide)
    first = lax.broadcasted_iota(jnp.int32, cosine.shape, 0) == 0
    scale = jnp.where(first, 1.0 / size, 2.0 / size)
    cosine, sine = cosine * scale, sine * scale
    response[0] = cosine
    response[1] = jnp.where(first, 0.0, sine)
    response[2] = jnp.where(first, sine, cosine)


def product(response, cosine, sine):
    wide = lambda which: jnp.concatenate([response[which]] * (cosine.shape[1] // LANE), axis=1)
    p, q, nyquist_p = wide(0), wide(1), wide(2)
    return cosine * p - sine * q, cosine * q + sine * nyquist_p


def kernel(
    tm_count, height_count,
    frames_hbm, tt_hbm, ht_hbm, tf_hbm, ti_hbm, hf_hbm, hi_hbm,
    out,
    frames, time_taps, height_taps, tf, ti, hf, hi, t_response, h_response,
    t_send, t_have, t_done, t_back, h_send, h_have, h_done, h_back,
    load_sems, send_sems, recv_sems,
):
    frames_dev, rows_dev, lane_total = frames.shape
    width = lane_total // CHUNKS
    groups = width // LANE
    block = frames_dev * rows_dev
    tm = lax.axis_index("tm")
    height = lax.axis_index("height")

    barrier = pltpu.get_barrier_semaphore()

    def tm_peer(d):
        return lax.rem(tm + d, tm_count)

    row, column, core = lax.div(height, 4), lax.rem(lax.div(height, 2), 2), lax.rem(height, 2)
    y_count = height_count // 4
    rows_at = [lax.rem(row + away, y_count) * 4 for away in range(y_count)]
    pairs_at = [(lax.rem(column + x, 2)) * 2 + lax.rem(core + c, 2) for x in (1, 0) for c in (1, 0)]
    by_hops = sorted(range(y_count), key=lambda away: -min(away, y_count - away))
    height_peers = [rows_at[y] + pairs_at[2 * x + c] for x in (0, 1) for y in by_hops for c in (0, 1)][:-1]

    def each_tm(act):
        act(tm_peer(tm_count // 2))

        def pair(m, carry):
            act(tm_peer(tm_count // 2 - m))
            act(tm_peer(tm_count // 2 + m))
            return carry

        lax.fori_loop(1, tm_count // 2, pair, 0)

    def each_height(act):
        for peer in height_peers:
            act(peer)

    each_tm(lambda peer: pl.semaphore_signal(barrier, inc=1, device_id=(peer, height), device_id_type=MESH))
    each_height(lambda peer: pl.semaphore_signal(barrier, inc=1, device_id=(tm, peer), device_id_type=MESH))

    loads = [
        pltpu.make_async_copy(src, dst, load_sems.at[i])
        for i, (src, dst) in enumerate([
            (frames_hbm, frames), (frames_hbm.at[:, :, pl.ds(width, width)], h_send.at[1]),
            (ht_hbm, height_taps), (hf_hbm, hf), (tt_hbm, time_taps), (tf_hbm, tf), (hi_hbm, hi), (ti_hbm, ti),
        ])
    ]
    for load in loads:
        load.start()

    loads[0].wait()
    swap_in = one_hot((block, block), lambda r, c: c == (r % frames_dev) * rows_dev + r // frames_dev)
    swap_back = one_hot((block, block), lambda r, c: c == (r % rows_dev) * frames_dev + r // rows_dev)

    def rows_first(values, c):
        flat = values.astype(F32).reshape(block, width).astype(BF16)
        turned = dot(swap_in, flat).astype(BF16)
        for g in range(groups):
            t_send[c, g * rows_dev:(g + 1) * rows_dev] = turned[:, g * LANE:(g + 1) * LANE].reshape(
                rows_dev, frames_dev, LANE
            )

    def frames_first(c, g):
        tile = t_back[c, g * rows_dev:(g + 1) * rows_dev].reshape(block, LANE)
        return dot(swap_back, tile).reshape(frames_dev, rows_dev, LANE)

    rows_first(frames[:, :, :width], 0)
    loads[1].wait()

    pl.semaphore_wait(barrier, tm_count + height_count - 2)

    def exchange_tm(phase, c, src, dst):
        each_tm(lambda peer: pltpu.make_async_remote_copy(
            src_ref=src.at[c, peer], dst_ref=dst.at[c, tm],
            send_sem=send_sems.at[phase, c], recv_sem=recv_sems.at[phase, c],
            device_id=(peer, height), device_id_type=MESH,
        ).start())
        pltpu.make_async_copy(src.at[c, tm], dst.at[c, tm], recv_sems.at[phase, c]).start()

    def from_home(c, first, last):
        def send(peer, carry):
            @pl.when(peer != tm)
            def _():
                pltpu.make_async_remote_copy(
                    src_ref=t_done.at[c, peer], dst_ref=t_back.at[c, tm],
                    send_sem=send_sems.at[1, c], recv_sem=recv_sems.at[1, c],
                    device_id=(peer, height), device_id_type=MESH,
                ).start()

            return carry

        lax.fori_loop(first, last, send, 0)

    def own_frames(c):
        pltpu.make_async_copy(t_done.at[c, tm], t_back.at[c, tm], recv_sems.at[1, c]).start()

    def exchange_height(phase, c, src, dst):
        each_height(lambda peer: pltpu.make_async_remote_copy(
            src_ref=src.at[c, peer], dst_ref=dst.at[c, height],
            send_sem=send_sems.at[phase, c], recv_sem=recv_sems.at[phase, c],
            device_id=(tm, peer), device_id_type=MESH,
        ).start())
        pltpu.make_async_copy(src.at[c, height], dst.at[c, height], recv_sems.at[phase, c]).start()

    def arrived(phase, c, dst):
        pltpu.make_async_copy(dst.at[c], dst.at[c], recv_sems.at[phase, c]).wait()

    def departed(phase, c, src, peers):
        sent = src.at[c, pl.ds(0, peers - 1)]
        pltpu.make_async_copy(sent, sent, send_sems.at[phase, c]).wait()

    def time_stage(c):
        arrived(0, c, t_have)
        values = t_have[c].reshape(tm_count * frames_dev, LANE)
        result = time_inverse(ti, *product(t_response, *time_forward(tf, values))).astype(BF16)
        t_done[c] = result.reshape(tm_count, frames_dev, LANE)
        own_frames(c)

    def height_stage(c):
        arrived(2, c, h_have)
        values = h_have[c].astype(F32).reshape(height_count * rows_dev, width).astype(BF16)
        result = height_inverse(hi, *product(h_response, *height_forward(hf, values)))
        h_done[c] = result.reshape(height_count, rows_dev, width).astype(BF16)
        exchange_height(3, c, h_done, h_back)

    exchange_height(2, 1, h_send, h_have)
    exchange_tm(0, 0, t_send, t_have)
    for load in loads[2:]:
        load.wait()
    store_response(height_forward, hf, height_taps, h_response)
    store_response(time_forward, tf, time_taps, t_response)

    early = EARLY_PLANES * 2

    def turn_to_height():
        arrived(1, 0, t_back)
        for g in range(groups):
            h_send[0, :, :, g * LANE:(g + 1) * LANE] = frames_first(0, g).astype(BF16)
        exchange_height(2, 0, h_send, h_have)

    height_stage(1)
    time_stage(0)
    from_home(0, 0, early)

    arrived(3, 1, h_back)
    rows_first(h_back[1], 1)
    exchange_tm(0, 1, t_send, t_have)
    from_home(0, early, tm_count)

    @pl.when(tm < early)
    def _():
        turn_to_height()

    height_first = jnp.logical_and(tm < 2, core == 0)

    @pl.when(height_first)
    def _():
        height_stage(0)

    time_stage(1)
    from_home(1, 0, tm_count)

    @pl.when(tm >= early)
    def _():
        turn_to_height()

    @pl.when(jnp.logical_not(height_first))
    def _():
        height_stage(0)

    arrived(3, 0, h_back)
    out[:, :, :width] = (frames[:, :, :width].astype(F32) + h_back[0].astype(F32)).astype(BF16)

    arrived(1, 1, t_back)
    for g in range(groups):
        lanes = slice(width + g * LANE, width + (g + 1) * LANE)
        out[:, :, lanes] = (frames[:, :, lanes].astype(F32) + frames_first(1, g)).astype(BF16)

    for c in range(CHUNKS):
        departed(0, c, t_send, tm_count)
        departed(1, c, t_done, tm_count)
        departed(2, c, h_send, height_count)
        departed(3, c, h_done, height_count)


def shards(frames_in, time_filter, height_filter):
    frames_dev, rows_dev, lane_total = frames_in.shape
    tm_count = lax.axis_size("tm")
    height_count = lax.axis_size("height")
    width = lane_total // CHUNKS
    tf, ti = time_tables(time_filter.shape[0])
    hf, hi = height_tables(height_filter.shape[0])
    t_buf = pltpu.VMEM((CHUNKS, tm_count, frames_dev, LANE), BF16)
    h_buf = pltpu.VMEM((CHUNKS, height_count, rows_dev, width), BF16)
    like = lambda a: pltpu.VMEM(a.shape, BF16)
    hbm = pl.BlockSpec(memory_space=pltpu.MemorySpace.HBM)
    vmem = pl.BlockSpec(memory_space=pltpu.VMEM)
    return pl.pallas_call(
        functools.partial(kernel, tm_count, height_count),
        out_shape=pltpu.VMEM(frames_in.shape, BF16),
        in_specs=[hbm] * 7,
        out_specs=vmem,
        scratch_shapes=[
            pltpu.VMEM(frames_in.shape, BF16),
            like(time_filter.T), like(height_filter.T), like(tf), like(ti), like(hf), like(hi),
            pltpu.VMEM((3, time_filter.shape[0] // 2, LANE), F32),
            pltpu.VMEM((3, height_filter.shape[0] // 2, LANE), F32),
            t_buf, t_buf, t_buf, t_buf, h_buf, h_buf, h_buf, h_buf,
            pltpu.SemaphoreType.DMA((8,)),
            pltpu.SemaphoreType.DMA((4, CHUNKS)),
            pltpu.SemaphoreType.DMA((4, CHUNKS)),
        ],
        compiler_params=pltpu.CompilerParams(collective_id=0, has_side_effects=True),
    )(frames_in, time_filter.T, height_filter.T, jnp.asarray(tf), jnp.asarray(ti), jnp.asarray(hf), jnp.asarray(hi))


def solution(mesh):
    return jax.shard_map(
        shards,
        mesh=mesh,
        in_specs=(P("tm", "height", None), P(), P()),
        out_specs=P("tm", "height", None),
        check_vma=False,
    )
```

```python
import functools

import jax
import jax.numpy as jnp
import numpy as np
from jax import lax
from jax.experimental import pallas as pl
from jax.experimental.pallas import tpu as pltpu
from jax.sharding import PartitionSpec as P

MESH = pl.DeviceIdType.MESH
F32, BF16 = jnp.float32, jnp.bfloat16
LANE = 128
CHUNKS = 2
EARLY_PLANES = 8


def split(table):
    high = table.astype(np.float32).astype(jnp.bfloat16)
    low = (table - high.astype(np.float64)).astype(np.float32).astype(jnp.bfloat16)
    return high, low


def dft_rows(size):
    half = size // 2
    order = np.concatenate([np.arange(0, half, 2), np.arange(1, half, 2)])
    angle = 2.0 * np.pi * ((order[:, None] * np.arange(size)[None, :]) % size) / size
    sines = np.sin(angle)
    sines[0] = np.cos(np.pi * np.arange(size))
    return np.cos(angle), sines


def time_tables(size):
    half, quarter = size // 2, size // 4
    cosines, sines = dft_rows(size)
    parts = [
        np.concatenate([cosines[rows, :half], sines[rows, :half]], axis=0)
        for rows in (slice(0, quarter), slice(quarter, half))
    ]
    forward = np.concatenate(split(np.concatenate(parts, axis=0)), axis=1)
    inverse = np.stack([piece for part in parts for piece in split(part.T)])
    return forward, inverse


def height_tables(size):
    high, low = split(np.concatenate(dft_rows(size), axis=0))
    return np.concatenate([high, low], axis=1), np.concatenate([high.T, low.T], axis=1)


def dot(a, b):
    return jnp.dot(a, b, preferred_element_type=F32)


def halves(values):
    high = values.astype(BF16)
    return high, (values - high.astype(F32)).astype(BF16)


def one_hot(shape, hit):
    rows = lax.broadcasted_iota(jnp.int32, shape, 0)
    cols = lax.broadcasted_iota(jnp.int32, shape, 1)
    return jnp.where(hit(rows, cols), 1.0, 0.0).astype(BF16)


def time_forward(table, values):
    half, quarter = values.shape[0] // 2, values.shape[0] // 4
    pair = jnp.concatenate([values[:half], values[half:]], axis=1)
    both = dot(table[...], jnp.concatenate([pair, pair], axis=0))
    even = both[:half, :LANE] + both[:half, LANE:]
    odd = both[half:, :LANE] - both[half:, LANE:]
    cosine = jnp.concatenate([even[:quarter], odd[:quarter]], axis=0)
    sine = jnp.concatenate([even[quarter:], odd[quarter:]], axis=0)
    return cosine, sine


def time_inverse(table, cosine, sine):
    quarter = cosine.shape[0] // 2
    sums = []
    for p in range(2):
        rows = slice(p * quarter, (p + 1) * quarter)
        high, low = halves(jnp.concatenate([cosine[rows], sine[rows]], axis=0))
        main = dot(table[2 * p], jnp.concatenate([high, low], axis=1))
        sums.append(main[:, :LANE] + main[:, LANE:] + dot(table[2 * p + 1], high))
    return jnp.concatenate([sums[0] + sums[1], sums[0] - sums[1]], axis=0)


def height_forward(table, values):
    half = values.shape[0] // 2
    both = dot(table[...], jnp.concatenate([values, values], axis=0))
    return both[:half], both[half:]


def height_inverse(table, cosine, sine):
    high, low = halves(jnp.concatenate([cosine, sine], axis=0))
    return dot(table[...], jnp.concatenate([high, high], axis=0)) + dot(table[:, :high.shape[0]], low)


def store_response(forward, table, taps, response):
    channels, size = taps.shape
    spread = one_hot((LANE, channels), lambda r, c: c == r % channels)
    wide = jnp.transpose(dot(spread, taps[...])).astype(BF16)
    cosine, sine = forward(table, wide)
    first = lax.broadcasted_iota(jnp.int32, cosine.shape, 0) == 0
    scale = jnp.where(first, 1.0 / size, 2.0 / size)
    cosine, sine = cosine * scale, sine * scale
    response[0] = cosine
    response[1] = jnp.where(first, 0.0, sine)
    response[2] = jnp.where(first, sine, cosine)


def product(response, cosine, sine):
    wide = lambda which: jnp.concatenate([response[which]] * (cosine.shape[1] // LANE), axis=1)
    p, q, nyquist_p = wide(0), wide(1), wide(2)
    return cosine * p - sine * q, cosine * q + sine * nyquist_p


def kernel(
    tm_count, height_count,
    frames_hbm, tt_hbm, ht_hbm, tf_hbm, ti_hbm, hf_hbm, hi_hbm,
    out,
    frames, time_taps, height_taps, tf, ti, hf, hi, t_response, h_response,
    t_send, t_have, t_done, t_back, h_send, h_have, h_done, h_back,
    load_sems, send_sems, recv_sems,
):
    frames_dev, rows_dev, lane_total = frames.shape
    width = lane_total // CHUNKS
    groups = width // LANE
    block = frames_dev * rows_dev
    tm = lax.axis_index("tm")
    height = lax.axis_index("height")

    barrier = pltpu.get_barrier_semaphore()

    def tm_peer(d):
        return lax.rem(tm + d, tm_count)

    row, column, core = lax.div(height, 4), lax.rem(lax.div(height, 2), 2), lax.rem(height, 2)
    y_count = height_count // 4
    rows_at = [lax.rem(row + away, y_count) * 4 for away in range(y_count)]
    pairs_at = [(lax.rem(column + x, 2)) * 2 + lax.rem(core + c, 2) for x in (1, 0) for c in (1, 0)]
    by_hops = sorted(range(y_count), key=lambda away: -min(away, y_count - away))
    height_peers = [rows_at[y] + pairs_at[2 * x + c] for x in (0, 1) for y in by_hops for c in (0, 1)][:-1]

    def each_tm(act):
        act(tm_peer(tm_count // 2))

        def pair(m, carry):
            act(tm_peer(tm_count // 2 - m))
            act(tm_peer(tm_count // 2 + m))
            return carry

        lax.fori_loop(1, tm_count // 2, pair, 0)

    def each_height(act):
        for peer in height_peers:
            act(peer)

    each_tm(lambda peer: pl.semaphore_signal(barrier, inc=1, device_id=(peer, height), device_id_type=MESH))
    each_height(lambda peer: pl.semaphore_signal(barrier, inc=1, device_id=(tm, peer), device_id_type=MESH))

    loads = [
        pltpu.make_async_copy(src, dst, load_sems.at[i])
        for i, (src, dst) in enumerate([
            (frames_hbm, frames), (frames_hbm.at[:, :, pl.ds(width, width)], h_send.at[1]),
            (ht_hbm, height_taps), (hf_hbm, hf), (tt_hbm, time_taps), (tf_hbm, tf), (hi_hbm, hi), (ti_hbm, ti),
        ])
    ]
    for load in loads:
        load.start()

    loads[0].wait()
    swap_in = one_hot((block, block), lambda r, c: c == (r % frames_dev) * rows_dev + r // frames_dev)
    swap_back = one_hot((block, block), lambda r, c: c == (r % rows_dev) * frames_dev + r // rows_dev)

    def rows_first(values, c):
        flat = values.astype(F32).reshape(block, width).astype(BF16)
        turned = dot(swap_in, flat).astype(BF16)
        for g in range(groups):
            t_send[c, g * rows_dev:(g + 1) * rows_dev] = turned[:, g * LANE:(g + 1) * LANE].reshape(
                rows_dev, frames_dev, LANE
            )

    def frames_first(c, g):
        tile = t_back[c, g * rows_dev:(g + 1) * rows_dev].reshape(block, LANE)
        return dot(swap_back, tile).reshape(frames_dev, rows_dev, LANE)

    rows_first(frames[:, :, :width], 0)
    loads[1].wait()

    pl.semaphore_wait(barrier, tm_count + height_count - 2)

    def exchange_tm(phase, c, src, dst):
        each_tm(lambda peer: pltpu.make_async_remote_copy(
            src_ref=src.at[c, peer], dst_ref=dst.at[c, tm],
            send_sem=send_sems.at[phase, c], recv_sem=recv_sems.at[phase, c],
            device_id=(peer, height), device_id_type=MESH,
        ).start())
        pltpu.make_async_copy(src.at[c, tm], dst.at[c, tm], recv_sems.at[phase, c]).start()

    def from_home(c, first, last):
        def send(peer, carry):
            @pl.when(peer != tm)
            def _():
                pltpu.make_async_remote_copy(
                    src_ref=t_done.at[c, peer], dst_ref=t_back.at[c, tm],
                    send_sem=send_sems.at[1, c], recv_sem=recv_sems.at[1, c],
                    device_id=(peer, height), device_id_type=MESH,
                ).start()

            return carry

        lax.fori_loop(first, last, send, 0)

    def own_frames(c):
        pltpu.make_async_copy(t_done.at[c, tm], t_back.at[c, tm], recv_sems.at[1, c]).start()

    def exchange_height(phase, c, src, dst):
        each_height(lambda peer: pltpu.make_async_remote_copy(
            src_ref=src.at[c, peer], dst_ref=dst.at[c, height],
            send_sem=send_sems.at[phase, c], recv_sem=recv_sems.at[phase, c],
            device_id=(tm, peer), device_id_type=MESH,
        ).start())
        pltpu.make_async_copy(src.at[c, height], dst.at[c, height], recv_sems.at[phase, c]).start()

    def arrived(phase, c, dst):
        pltpu.make_async_copy(dst.at[c], dst.at[c], recv_sems.at[phase, c]).wait()

    def departed(phase, c, src, peers):
        sent = src.at[c, pl.ds(0, peers - 1)]
        pltpu.make_async_copy(sent, sent, send_sems.at[phase, c]).wait()

    def time_stage(c):
        arrived(0, c, t_have)
        values = t_have[c].reshape(tm_count * frames_dev, LANE)
        result = time_inverse(ti, *product(t_response, *time_forward(tf, values))).astype(BF16)
        t_done[c] = result.reshape(tm_count, frames_dev, LANE)
        own_frames(c)

    def height_stage(c):
        arrived(2, c, h_have)
        values = h_have[c].astype(F32).reshape(height_count * rows_dev, width).astype(BF16)
        result = height_inverse(hi, *product(h_response, *height_forward(hf, values)))
        h_done[c] = result.reshape(height_count, rows_dev, width).astype(BF16)
        exchange_height(3, c, h_done, h_back)

    exchange_tm(0, 0, t_send, t_have)
    exchange_height(2, 1, h_send, h_have)
    for load in loads[2:]:
        load.wait()
    store_response(height_forward, hf, height_taps, h_response)
    store_response(time_forward, tf, time_taps, t_response)

    early = EARLY_PLANES * 2

    def turn_to_height():
        arrived(1, 0, t_back)
        for g in range(groups):
            h_send[0, :, :, g * LANE:(g + 1) * LANE] = frames_first(0, g).astype(BF16)
        exchange_height(2, 0, h_send, h_have)

    height_stage(1)
    time_stage(0)
    from_home(0, 0, early)

    arrived(3, 1, h_back)
    rows_first(h_back[1], 1)
    exchange_tm(0, 1, t_send, t_have)
    from_home(0, early, tm_count)

    @pl.when(tm < early)
    def _():
        turn_to_height()

    height_first = jnp.logical_and(tm < 2, core == 0)

    @pl.when(height_first)
    def _():
        height_stage(0)

    time_stage(1)
    from_home(1, 0, tm_count)

    @pl.when(tm >= early)
    def _():
        turn_to_height()

    @pl.when(jnp.logical_not(height_first))
    def _():
        height_stage(0)

    arrived(3, 0, h_back)
    out[:, :, :width] = (frames[:, :, :width].astype(F32) + h_back[0].astype(F32)).astype(BF16)

    arrived(1, 1, t_back)
    for g in range(groups):
        lanes = slice(width + g * LANE, width + (g + 1) * LANE)
        out[:, :, lanes] = (frames[:, :, lanes].astype(F32) + frames_first(1, g)).astype(BF16)

    for c in range(CHUNKS):
        departed(0, c, t_send, tm_count)
        departed(1, c, t_done, tm_count)
        departed(2, c, h_send, height_count)
        departed(3, c, h_done, height_count)


def shards(frames_in, time_filter, height_filter):
    frames_dev, rows_dev, lane_total = frames_in.shape
    tm_count = lax.axis_size("tm")
    height_count = lax.axis_size("height")
    width = lane_total // CHUNKS
    tf, ti = time_tables(time_filter.shape[0])
    hf, hi = height_tables(height_filter.shape[0])
    t_buf = pltpu.VMEM((CHUNKS, tm_count, frames_dev, LANE), BF16)
    h_buf = pltpu.VMEM((CHUNKS, height_count, rows_dev, width), BF16)
    like = lambda a: pltpu.VMEM(a.shape, BF16)
    hbm = pl.BlockSpec(memory_space=pltpu.MemorySpace.HBM)
    vmem = pl.BlockSpec(memory_space=pltpu.VMEM)
    return pl.pallas_call(
        functools.partial(kernel, tm_count, height_count),
        out_shape=pltpu.VMEM(frames_in.shape, BF16),
        in_specs=[hbm] * 7,
        out_specs=vmem,
        scratch_shapes=[
            pltpu.VMEM(frames_in.shape, BF16),
            like(time_filter.T), like(height_filter.T), like(tf), like(ti), like(hf), like(hi),
            pltpu.VMEM((3, time_filter.shape[0] // 2, LANE), F32),
            pltpu.VMEM((3, height_filter.shape[0] // 2, LANE), F32),
            t_buf, t_buf, t_buf, t_buf, h_buf, h_buf, h_buf, h_buf,
            pltpu.SemaphoreType.DMA((8,)),
            pltpu.SemaphoreType.DMA((4, CHUNKS)),
            pltpu.SemaphoreType.DMA((4, CHUNKS)),
        ],
        compiler_params=pltpu.CompilerParams(collective_id=0, has_side_effects=True),
    )(frames_in, time_filter.T, height_filter.T, jnp.asarray(tf), jnp.asarray(ti), jnp.asarray(hf), jnp.asarray(hi))


def solution(mesh):
    return jax.shard_map(
        shards,
        mesh=mesh,
        in_specs=(P("tm", "height", None), P(), P()),
        out_specs=P("tm", "height", None),
        check_vma=False,
    )
```
